128 devices in a mesh: event: 4 (over z), terrain: 32 (over y, x, core).
Axes of the slice: x: 4, y: 4, z: 4, core: 2. Of those that a mesh axis runs over, the one named last changes fastest.
Arguments:
- level_start: float32 [4, 1024, 1024], P('event', 'terrain'), may hold values from -18 to 18
- bed_depth: float32 [1024, 1024], P('terrain'), may hold values from 0.5 to 2
- wet_bits: int32 [4, 1024, 1024], P('event', 'terrain'), may hold values from 0 to 255
- tile_owner: int32 [8192, 1], P('terrain'), may hold values from 0 to 31; in each aligned block of 256 rows (0 to 255, 256 to 511, ...) at most 12 rows name the same one
- vuln_weight: bfloat16 [128, 256], replicated, may hold values from -0.5 to 0.5
- vuln_bias: float32 [256], replicated, may hold values from -2 to 2
- account_index: int32 [12288, 128], P('terrain'), may hold values from 0 to 1023
- bin_index: int32 [12288, 128], P('terrain'), may hold values from 0 to 255
- exposure_value: bfloat16 [12288, 128], P('terrain'), may hold values from 1 to 10
- deductible: float32 [1024], replicated, may hold values from 0 to 0.8
- limit: float32 [1024], replicated, may hold values from 0.5 to 1.5
Outputs:
- level: float32 [4, 1024, 1024], P('event', 'terrain')
- net_loss: bfloat16 [4, 1024, 256], P('event')
- portfolio: float32 [1024, 256], P('terrain')
The draws below stay inside these ranges and needn't reach their ends.
Inputs may be any that keep to these rules, and one draw needn't show every extreme that they name: `tile_owner`: among the 256 tiles of one device no owner is named more than 12 times; in some devices one owner is named exactly 12 times. `wet_bits`: bit s (the value // 2**s, mod 2) is 1 where the cell is wet in substep s. `account_index`: rows of an owner's records that no tile reaches are not read.
All inputs are finite; a program needn't handle non-finite values.
Results may differ from the reference program's by a relative error of at most 0.0004.
The reference program's roundings to bfloat16 on the way (of `pieces` and `ratio`) count: a program that leaves them out, or rounds other values in their place, can miss the bound.
Values may be sent and summed in bfloat16 or wider, within the bound.
No kernel may reach another device: no remote copies, remote signals or barrier semaphores. Data moves between devices by JAX's collectives and lax.ppermute only.
A program may use at most 64 MiB of HBM per device.

```python
import math
import jax
import jax.numpy as jnp
import numpy as np
from jax import lax

NY = 1024
TILE = 128
BINS = 256
ACCOUNTS = 1024
SUBSTEPS = 8
GROUPS = 4
ROWS = 1024
TILES_DEV = 256
TILES = 8192
CAP = 12
SLOTS = 384
N_TERRAIN = 32


def set_ends(array, stream_key, least, top_value):
    longest = array.shape.index(max(array.shape))
    spots = []
    for shift in (0, 1):
        where = [jax.random.randint(jax.random.fold_in(stream_key, axis), (), 0, length) for axis, length in enumerate(array.shape)]
        where[longest] = (where[longest] + shift) % array.shape[longest]
        spots.append(tuple(where))
    return array.at[spots[0]].set(least).at[spots[1]].set(top_value)


def level_of(stream_key, extent, shards, low, top_value):
    loudness, own = 1.0, jax.random.fold_in(stream_key, 6)
    for dim, shards_of in shards:
        draws = jnp.exp(jax.random.uniform(jax.random.fold_in(own, dim), (shards_of,), jnp.float32, low / len(shards), top_value / len(shards)))
        loudness = loudness * jnp.repeat(draws, extent[dim] // shards_of).reshape([-1 if axis == dim else 1 for axis in range(len(extent))])
    return loudness


def routed_block(stream_key, own, number, rows, count, top, bound, lean):
    order = jax.random.permutation(stream_key, count)
    packed, common = shares(count, rows * top, bound, lean, True), shares(count, rows * top, bound, lean, False)
    places = jnp.arange(count)

    def named(lengths, offset_by):
        used = int((lengths > 0).sum())
        fixed = max(1, used // 4)
        passed = fixed + (places - fixed + offset_by * (used - fixed)) % max(1, count - fixed)
        return jnp.zeros((count,), jnp.int32).at[order[jnp.where(places < fixed, places, passed)]].set(jnp.asarray(lengths, jnp.int32))

    lengths = jnp.where(number % 4 == 0, named(packed, number // 4), named(common, number - number // 4 - 1))
    mixed = jax.random.permutation(jax.random.fold_in(own, 3), count)
    donor, sink = mixed[0:count // 2 * 2:2], mixed[1:count // 2 * 2:2]
    room = jnp.minimum(lengths[donor] - 1, bound - lengths[sink]) // 2
    room = jnp.where((donor == order[0]) | (sink == order[0]) | (lengths[sink] == 0), 0, jnp.maximum(room, 0))
    passed = jax.random.randint(jax.random.fold_in(own, 4), (count // 2,), 0, 1 << 20) % (room + 1)
    lengths = lengths.at[donor].add(-passed).at[sink].add(passed)
    items = jnp.searchsorted(jnp.cumsum(lengths), jnp.arange(rows * top), side="right").astype(jnp.int32)
    table = items.reshape(top, rows).T
    table = table[jax.random.permutation(jax.random.fold_in(own, 1), rows)]
    offset_by = jax.random.randint(jax.random.fold_in(own, 2), (rows, 1), 0, top)
    return jnp.take_along_axis(table, (jnp.arange(top)[None, :] + offset_by) % top, axis=1)


def shares(number_of, total, most, lean, full):
    loads = [(1 << 20) // math.isqrt(grade ** lean) + 1 for grade in range(1, number_of + 1)]
    largest = most if full else min(most, max(-(-total // number_of), total * loads[0] // sum(loads)))
    least = 1 if total - largest >= number_of - 1 else 0
    holding, spare = [largest] + [least] * (number_of - 1), total - largest - least * (number_of - 1)
    while spare > 0:
        candidates = [i for i in range(1, number_of) if holding[i] < largest] or [i for i in range(1, number_of) if holding[i] < most]
        whole, remaining = sum([loads[i] for i in candidates]), spare
        for i in candidates:
            addition = min(most - holding[i], max(1, remaining * loads[i] // whole), spare)
            holding[i] = holding[i] + addition
            spare = spare - addition
    return np.array(holding)


def bell_draw(own_key, shape, width, reach, split=(), held_as=jnp.bfloat16):
    loudness = level_of(own_key, shape, split, -0.22, 0.18) if split else 1.0
    result = jax.random.normal(own_key, shape, jnp.float32) * width * loudness
    return jnp.minimum(jnp.maximum(result, -reach), reach).astype(held_as)


def setup_inputs(seed: int = 0) -> dict:
    splits = jax.random.split(jax.random.key(seed), 12)
    level_start = bell_draw(splits[0], (GROUPS, ROWS, NY), 3.0, 18.0, ((0, 4), (1, 32)), jnp.float32)
    bed_depth = jnp.clip(jnp.exp(math.log(2.0) - 1.3862944 * jax.random.uniform(splits[1], (ROWS, NY), jnp.float32) ** level_of(splits[1], (ROWS, NY), ((0, 32),), -0.2, 0.2)), 0.5, 2.0)
    wet_bits = set_ends(jax.random.randint(splits[2], (GROUPS, ROWS, NY), 0, 2 ** SUBSTEPS), jax.random.fold_in(splits[2], 1), 0, (2 ** SUBSTEPS) - 1).astype(jnp.int32)
    tile_owner_keys = jax.random.split(jax.random.fold_in(splits[3], 1), TILES // TILES_DEV)
    tile_owner_turns = jax.random.permutation(jax.random.fold_in(splits[3], 3), TILES // TILES_DEV)
    tile_owner = jax.vmap(lambda own, number: routed_block(jax.random.fold_in(splits[3], 2), own, number, TILES_DEV, N_TERRAIN, 1, CAP, 2))(tile_owner_keys, tile_owner_turns).reshape((TILES, 1))
    vuln_weight = bell_draw(splits[4], (TILE, BINS), TILE ** -0.5, 0.5)
    vuln_bias = jnp.clip(jax.random.uniform(splits[5], (BINS,), jnp.float32, -2.0, 2.0), -2.0, 2.0)
    account_index = set_ends(jax.random.randint(splits[6], (N_TERRAIN * SLOTS, TILE), 0, ACCOUNTS), jax.random.fold_in(splits[6], 1), 0, ACCOUNTS - 1).astype(jnp.int32)
    bin_index = set_ends(jax.random.randint(splits[7], (N_TERRAIN * SLOTS, TILE), 0, BINS), jax.random.fold_in(splits[7], 1), 0, BINS - 1).astype(jnp.int32)
    exposure_value = jnp.clip(jnp.exp(math.log(10.0) - 2.3025851 * jax.random.uniform(splits[8], (N_TERRAIN * SLOTS, TILE), jnp.float32) ** level_of(splits[8], (N_TERRAIN * SLOTS, TILE), ((0, 32),), -0.2, 0.2)), 1.0, 10.0).astype(jnp.bfloat16)
    deductible = jnp.clip(jax.random.uniform(splits[9], (ACCOUNTS,), jnp.float32, 0.0, 0.8), 0.0, 0.8)
    limit = jnp.clip(jax.random.uniform(splits[10], (ACCOUNTS,), jnp.float32, 0.5, 1.5), 0.5, 1.5)
    return dict(level_start=level_start, bed_depth=bed_depth, wet_bits=wet_bits, tile_owner=tile_owner, vuln_weight=vuln_weight, vuln_bias=vuln_bias, account_index=account_index, bin_index=bin_index, exposure_value=exposure_value, deductible=deductible, limit=limit)


courant = 0.5
gravity = 1.0


def pad_columns(field):
    return jnp.pad(field[:, 1:-1, :], ((0, 0), (0, 0), (1, 1)))


def neighbour_mean(field):
    inner = pad_columns(field)
    return 0.25 * (field[:, 2:, :] + field[:, :-2, :] + inner[:, :, 2:] + inner[:, :, :-2])


def friedrichs_step(level, row_speed, col_speed, bed_depth, wet_factor):
    row_flow = bed_depth * row_speed
    col_flow = pad_columns(bed_depth * col_speed)
    level_pad = pad_columns(level)
    new_level = neighbour_mean(level) - 0.5 * courant * ((row_flow[:, 2:, :] - row_flow[:, :-2, :]) + (col_flow[:, :, 2:] - col_flow[:, :, :-2]))
    new_row = (neighbour_mean(row_speed) - 0.5 * courant * gravity * (level[:, 2:, :] - level[:, :-2, :])) * wet_factor
    new_col = (neighbour_mean(col_speed) - 0.5 * courant * gravity * (level_pad[:, :, 2:] - level_pad[:, :, :-2])) * wet_factor
    return new_level, new_row, new_col


def pad_rows(field):
    return jnp.pad(field, ((0, 0), (1, 1), (0, 0)))


def reference(level_start, bed_depth, wet_bits, tile_owner, vuln_weight, vuln_bias, account_index, bin_index, exposure_value, deductible, limit):
    level = level_start
    row_speed = jnp.zeros_like(level_start)
    col_speed = jnp.zeros_like(level_start)
    bed_pad = jnp.pad(bed_depth, ((1, 1), (0, 0)))
    for step in range(SUBSTEPS):
        wet_factor = ((wet_bits // (2 ** step)) % 2).astype(jnp.float32)
        level, row_speed, col_speed = friedrichs_step(pad_rows(level), pad_rows(row_speed), pad_rows(col_speed), bed_pad, wet_factor)
    pieces = level.astype(jnp.bfloat16).reshape(GROUPS, TILES, TILE)
    owner = tile_owner[:, 0].reshape(N_TERRAIN, TILES_DEV)
    onehot = (owner[:, :, None] == jnp.arange(N_TERRAIN, dtype=jnp.int32)[None, None, :]).astype(jnp.int32)
    rank = jnp.sum((jnp.cumsum(onehot, axis=1) - onehot) * onehot, axis=2)
    source = jnp.arange(N_TERRAIN, dtype=jnp.int32)[:, None]
    record = (owner * SLOTS + source * CAP + rank).reshape(TILES).astype(jnp.int32)
    accounts = account_index[record]
    thresholds = bin_index[record]
    values = exposure_value[record]
    block = math.gcd(TILES, 256)
    bin_range = jnp.arange(BINS, dtype=jnp.int32)

    def group_loss(tiles_group):
        ratio = jax.nn.sigmoid(jnp.dot(tiles_group, vuln_weight, preferred_element_type=jnp.float32) + vuln_bias).astype(jnp.bfloat16)

        def add_block(total, block_id):
            start = (block_id * block).astype(jnp.int32)
            ratio_part = lax.dynamic_slice_in_dim(ratio, start, block, 0).astype(jnp.float32)
            account_part = lax.dynamic_slice_in_dim(accounts, start, block, 0)
            threshold_part = lax.dynamic_slice_in_dim(thresholds, start, block, 0)
            value_part = lax.dynamic_slice_in_dim(values, start, block, 0).astype(jnp.float32)
            inside = (bin_range[None, None, :] >= threshold_part[:, :, None]).astype(jnp.float32)
            weight = value_part[:, :, None] * ratio_part[:, None, :] * inside
            total = total + jax.ops.segment_sum(weight.reshape(-1, BINS), account_part.reshape(-1), num_segments=ACCOUNTS)
            return total, None

        total, _ = lax.scan(add_block, jnp.zeros((ACCOUNTS, BINS), jnp.float32), jnp.arange(TILES // block, dtype=jnp.int32))
        return total

    gross = lax.map(group_loss, pieces)
    scaled = gross * (ACCOUNTS / (ROWS * NY))
    net = jnp.minimum(jnp.maximum(scaled - deductible[None, :, None], 0.0), limit[None, :, None])
    portfolio = jnp.sum(net, axis=0) / GROUPS
    return level, net.astype(jnp.bfloat16), portfolio
```

```python
import functools

import jax
import jax.numpy as jnp
from jax import lax
from jax.experimental import pallas as pl
from jax.experimental.pallas import tpu as pltpu
from jax.sharding import PartitionSpec as P

SUBSTEPS = 8
HALO = 8
f32 = jnp.float32
bf16 = jnp.bfloat16


def shifted_columns(ahead, behind):
    width = ahead.shape[1]
    right = pltpu.roll(ahead, width - 1, axis=1)
    left = pltpu.roll(behind, 1, axis=1)
    lane = lax.broadcasted_iota(jnp.int32, (ahead.shape[0], 128), 1)
    right = jnp.concatenate(
        [right[:, : width - 128], jnp.where(lane == 127, 0.0, right[:, width - 128 :])], axis=1
    )
    left = jnp.concatenate([jnp.where(lane == 0, 0.0, left[:, :128]), left[:, 128:]], axis=1)
    return right + left


def shifted_rows(ahead, behind):
    count = ahead.shape[0]
    return pltpu.roll(ahead, count - 1, axis=0) + pltpu.roll(behind, 1, axis=0)


def water_kernel(own, mate, edge_a, edge_b, weight, bias, level_out, ratio_out, level, row, col, bed, wet, mask, *, rows):
    odd = lax.axis_index("terrain") % 2 == 1
    for place, target in enumerate((level, bed, wet)):
        mine = own[place * rows : (place + 1) * rows]
        other = mate[place * rows : (place + 1) * rows]
        a = edge_a[place * HALO : (place + 1) * HALO]
        b = edge_b[place * HALO : (place + 1) * HALO]
        pick = [
            jnp.where(odd, b, a),
            jnp.where(odd, other, mine),
            jnp.where(odd, mine, other),
            jnp.where(odd, a, b),
        ]
        whole = jnp.concatenate(pick, axis=0)
        if target is wet:
            whole = whole.astype(jnp.int32)
        if target is bed:
            mask[...] = (whole > 0.0).astype(f32)
        target[...] = whole
    row[...] = jnp.zeros_like(row)
    col[...] = jnp.zeros_like(col)

    def substep(step, _):
        l, r, c, d = level[...], row[...], col[...], bed[...]
        factor = (lax.shift_right_logical(wet[...], step) & 1).astype(f32)
        rf, cf = d * r, d * c
        level[...] = 0.25 * (shifted_rows(l - rf, l + rf) + shifted_columns(l - cf, l + cf)) * mask[...]
        row[...] = 0.25 * (shifted_rows(r - l, r + l) + shifted_columns(r, r)) * factor
        col[...] = 0.25 * (shifted_rows(c, c) + shifted_columns(c - l, c + l)) * factor
        return 0

    lax.fori_loop(0, SUBSTEPS, substep, 0)
    level_out[...] = jnp.where(odd, level[HALO + rows : HALO + 2 * rows], level[HALO : HALO + rows])
    pieces = level[HALO : HALO + 2 * rows].astype(bf16)
    cells = weight.shape[0]
    w = weight[...]
    half = w.shape[1] // 2
    for j in range(pieces.shape[1] // cells):
        z = jnp.dot(pieces[:, j * cells : (j + 1) * cells], w, preferred_element_type=f32) + bias[...]
        ratio = jax.nn.sigmoid(z).astype(bf16).astype(f32)
        span = slice(j * 2 * rows, (j + 1) * 2 * rows)
        ratio_out[0, span] = ratio[:, :half]
        ratio_out[1, span] = ratio[:, half:]


def gross_kernel(place, records, ratio, out, rows, bins, bins_t, left, right, *, group, per_row, tiles):
    odd = lax.axis_index("terrain") % 2
    senders, triple, cells = records.shape
    each = triple // 3

    def unpack(sender, _):
        block = records[sender].astype(jnp.int32)
        account = block[:each]
        number = jnp.where(
            ((account >> 4) & 1) == odd, ((account >> 5) << 4) | (account & 15), 4095
        )
        low = jnp.where(number < 256, number, -1)
        high = jnp.where((number >= 256) & (number < 512), number - 256, -1)
        span = pl.ds(pl.multiple_of(sender * each, each), each)
        rows[0, span] = low.astype(f32)
        rows[1, span] = high.astype(f32)
        rows[2, span] = block[2 * each :].astype(f32) * (1 / 128)
        rows[3, span] = block[each : 2 * each].astype(f32)
        return 0

    lax.fori_loop(0, senders, unpack, 0)
    strip_rows = tiles // (2 * per_row)
    per_col = 2 * strip_rows // 8

    def tile_of(eight, u):
        j = eight // per_col
        i = (eight % per_col) * 8 + u
        return (i // strip_rows) * (tiles // 2) + (i % strip_rows) * per_row + j

    def gather(eight, _):
        for u in range(8):
            bins[pl.ds(eight * 8 + u, 1), :] = rows[3, pl.ds(place[tile_of(eight, u)], 1), :]
        return 0

    lax.fori_loop(0, tiles // 8, gather, 0)
    for k in range(tiles // 128):
        bins_t[k] = bins[k * 128 : (k + 1) * 128, :].T
    out[...] = jnp.zeros_like(out)
    number = lax.broadcasted_iota(jnp.int32, (256, cells), 0).astype(f32).astype(bf16)
    first_bins = lax.broadcasted_iota(jnp.int32, (cells, 128), 1).astype(f32).astype(bf16)
    last_bins = (lax.broadcasted_iota(jnp.int32, (cells, 128), 1) + 128).astype(f32).astype(bf16)
    no_left = jnp.zeros((256, cells), bf16)
    no_right = jnp.zeros((cells, 128), bf16)

    def spread(row, count):
        packed = jnp.broadcast_to(row, (16, 128)).astype(bf16)
        return jnp.concatenate([packed] * (count // 16), axis=0)

    def build(block, slot):
        for x in range(group // 8):
            eight = block * (group // 8) + x
            shown = pltpu.roll(bins_t[eight // 16], (128 - 8 * (eight % 16)) % 128, axis=1)
            for u in range(8):
                w = x * 8 + u
                record = place[tile_of(eight, u)]
                low, high, value = [spread(rows[k, pl.ds(record, 1), :], 256) for k in range(3)]
                left[slot, w, :256] = jnp.where(low == number, value, no_left)
                left[slot, w, 256:] = jnp.where(high == number, value, no_left)
                bin_of = jnp.broadcast_to(shown[:, u : u + 1], (cells, 128)).astype(bf16)
                for k, these in enumerate((first_bins, last_bins)):
                    some = spread(ratio[k, pl.ds(eight * 8 + u, 1), :], cells)
                    right[slot, k, w * cells : (w + 1) * cells] = jnp.where(these >= bin_of, some, no_right)

    def add(slot):
        l = jnp.concatenate([left[slot, w] for w in range(group)], axis=1)
        r = jnp.concatenate([right[slot, 0], right[slot, 1]], axis=1)
        out[...] += jnp.dot(l, r, preferred_element_type=f32)

    blocks = tiles // group
    build(0, 0)

    def pair(m, _):
        build(2 * m + 1, 1)
        add(0)
        build(jnp.minimum(2 * m + 2, blocks - 1), 0)
        add(1)
        return 0

    lax.fori_loop(0, blocks // 2, pair, 0)


def per_device(
    level_start,
    bed_depth,
    wet_bits,
    tile_owner,
    vuln_weight,
    vuln_bias,
    account_index,
    bin_index,
    exposure_value,
    deductible,
    limit,
):
    _, rows, width = level_start.shape
    cells, bin_count = vuln_weight.shape
    account_count = deductible.shape[0]
    owners = lax.axis_size("terrain")
    events = lax.axis_size("event")
    me = lax.axis_index("terrain")
    odd = me % 2 == 1
    slots = account_index.shape[0]
    capacity = slots // owners
    tiles = tile_owner.shape[0]
    vmem = pl.BlockSpec(memory_space=pltpu.VMEM)

    in_pairs = lambda x: x.astype(jnp.int16).reshape(owners // 2, 2 * capacity, cells)
    records = jnp.concatenate(
        [in_pairs(account_index), in_pairs(bin_index), in_pairs(exposure_value.astype(f32) * 128.0)],
        axis=1,
    )
    records = jnp.repeat(records, 2, axis=0)
    records = lax.all_to_all(records, "terrain", 0, 0, tiled=True)

    level_in, wet_in = level_start[0], wet_bits[0].astype(f32)
    owner_row = jnp.pad(tile_owner.reshape(1, tiles).astype(f32), ((0, 7), (0, width - tiles)))
    own = jnp.concatenate([level_in, bed_depth, wet_in, owner_row], axis=0)
    edge = jnp.concatenate(
        [jnp.where(odd, x[rows - HALO :], x[:HALO]) for x in (level_in, bed_depth, wet_in)], axis=0
    )
    mate = lax.ppermute(own, "terrain", [(i, i ^ 1) for i in range(owners)])

    def outward(step):
        pairs = [(i, i + step if i % 2 else i - step) for i in range(owners)]
        return [(i, k) for i, k in pairs if 0 <= k < owners]

    edge_a = lax.ppermute(edge, "terrain", outward(1))
    edge_b = lax.ppermute(edge, "terrain", outward(2))

    level, ratio = pl.pallas_call(
        functools.partial(water_kernel, rows=rows),
        in_specs=[vmem] * 6,
        out_specs=(vmem, vmem),
        out_shape=(
            jax.ShapeDtypeStruct((rows, width), f32),
            jax.ShapeDtypeStruct((2, 2 * tiles, bin_count // 2), f32),
        ),
        scratch_shapes=[pltpu.VMEM((2 * (rows + HALO), width), f32)] * 4
        + [pltpu.VMEM((2 * (rows + HALO), width), jnp.int32), pltpu.VMEM((2 * (rows + HALO), width), f32)],
        compiler_params=pltpu.CompilerParams(vmem_limit_bytes=32 << 20),
        name="water",
    )(own, mate, edge_a, edge_b, vuln_weight, vuln_bias[None])

    owner_pair = jnp.stack([own[3 * rows, :tiles], mate[3 * rows, :tiles]])
    owner_pair = jnp.where(odd, owner_pair[::-1], owner_pair).astype(jnp.int32)
    order = jnp.arange(tiles, dtype=jnp.int32)
    same = (owner_pair[:, :, None] == owner_pair[:, None, :]) & (order[:, None] < order[None, :])
    rank = jnp.sum(same.astype(jnp.int32), axis=1)
    place = owner_pair * (2 * capacity) + jnp.array([[0], [1]], jnp.int32) * capacity + rank

    group = 16
    share = account_count // owners
    half_share = share // 2
    gross = pl.pallas_call(
        functools.partial(gross_kernel, group=group, per_row=width // cells, tiles=2 * tiles),
        grid_spec=pltpu.PrefetchScalarGridSpec(
            num_scalar_prefetch=1,
            grid=(),
            in_specs=[vmem, vmem],
            out_specs=vmem,
            scratch_shapes=[
                pltpu.VMEM((4, owners * 2 * capacity, cells), f32),
                pltpu.VMEM((2 * tiles, cells), f32),
                pltpu.VMEM((2 * tiles // 128, cells, 128), f32),
                pltpu.VMEM((2, group, account_count // 2, cells), bf16),
                pltpu.VMEM((2, 2, group * cells, bin_count // 2), bf16),
            ],
        ),
        out_shape=jax.ShapeDtypeStruct((account_count // 2, bin_count), f32),
        compiler_params=pltpu.CompilerParams(vmem_limit_bytes=40 << 20),
        name="gross",
    )(place.reshape(-1), records, ratio)

    parts = lax.all_to_all(gross.reshape(owners, half_share, bin_count), "terrain", 0, 0, tiled=True)
    own_gross = parts.reshape(owners // 2, 2, half_share, bin_count).sum(axis=0).reshape(share, bin_count)
    scale = account_count / (rows * owners * width)
    own_deduct = lax.dynamic_slice_in_dim(deductible, me * share, share, 0)
    own_limit = lax.dynamic_slice_in_dim(limit, me * share, share, 0)
    net = jnp.minimum(jnp.maximum(own_gross * scale - own_deduct[:, None], 0.0), own_limit[:, None])
    everyone = jnp.broadcast_to(net.astype(bf16)[None], (owners, share, bin_count))
    net_loss = lax.all_to_all(everyone, "terrain", 0, 0, tiled=True).reshape(1, account_count, bin_count)
    others = [
        lax.ppermute(net, "event", [(i, (i + k) % events) for i in range(events)])
        for k in range(1, events)
    ]
    portfolio = sum(others, net) / events
    return (level[None], net_loss, portfolio)


def solution(mesh):
    placed = (
        P("event", "terrain", None),
        P("terrain", None),
        P("event", "terrain", None),
        P("terrain", None),
        P(),
        P(),
        P("terrain", None),
        P("terrain", None),
        P("terrain", None),
        P(),
        P(),
    )
    return jax.shard_map(
        per_device,
        mesh=mesh,
        in_specs=placed,
        out_specs=(P("event", "terrain", None), P("event", None, None), P("terrain", None)),
        check_vma=False,
    )
```

```python
import functools

import jax
import jax.numpy as jnp
from jax import lax
from jax.experimental import pallas as pl
from jax.experimental.pallas import tpu as pltpu
from jax.sharding import PartitionSpec as P

SUBSTEPS = 8
HALO = 8
f32 = jnp.float32
bf16 = jnp.bfloat16


def shifted_columns(ahead, behind):
    width = ahead.shape[1]
    right = pltpu.roll(ahead, width - 1, axis=1)
    left = pltpu.roll(behind, 1, axis=1)
    lane = lax.broadcasted_iota(jnp.int32, (ahead.shape[0], 128), 1)
    right = jnp.concatenate(
        [right[:, : width - 128], jnp.where(lane == 127, 0.0, right[:, width - 128 :])], axis=1
    )
    left = jnp.concatenate([jnp.where(lane == 0, 0.0, left[:, :128]), left[:, 128:]], axis=1)
    return right + left


def shifted_rows(ahead, behind):
    count = ahead.shape[0]
    return pltpu.roll(ahead, count - 1, axis=0) + pltpu.roll(behind, 1, axis=0)


def pack_kernel(*refs, each):
    sources, (records, own, edge), held, arrived = refs[:7], refs[7:10], refs[10:17], refs[17]
    copies = [pltpu.make_async_copy(x, y, arrived.at[k]) for k, (x, y) in enumerate(zip(sources, held))]
    for copy in copies:
        copy.start()
    account, bins, value, level, bed, wet, owner = held
    odd = lax.axis_index("terrain") % 2 == 1
    for copy in copies[:3]:
        copy.wait()

    def two_pairs(two, _):
        span = pl.ds(pl.multiple_of(two * 2 * each, 2 * each), 2 * each)
        parts = (account[span], bins[span], (value[span].astype(f32) * 128.0).astype(jnp.int32))
        for k, part in enumerate(parts):
            for pair in range(2):
                block = part[pair * each : (pair + 1) * each].astype(jnp.int16)
                for core in range(2):
                    records[two * 4 + pair * 2 + core, k * each : (k + 1) * each] = block
        return 0

    lax.fori_loop(0, records.shape[0] // 4, two_pairs, 0)
    for copy in copies[3:]:
        copy.wait()
    rows = level.shape[0]
    for k, field in enumerate((level[...], bed[...], wet[...].astype(f32))):
        own[k * rows : (k + 1) * rows] = field
        edge[k * HALO : (k + 1) * HALO] = jnp.where(odd, field[rows - HALO :], field[:HALO])
    own[3 * rows :] = jnp.zeros((own.shape[0] - 3 * rows, own.shape[1]), f32)
    own[3 * rows : 3 * rows + 1, : owner.shape[1]] = owner[...].astype(f32)


def ranks_of(owner):
    blocks = [owner[:, k : k + 128] for k in range(0, owner.shape[1], 128)]
    down = [jnp.broadcast_to(x, (128, 128)).T for x in blocks]
    earlier = lax.broadcasted_iota(jnp.int32, (128, 128), 0) < lax.broadcasted_iota(jnp.int32, (128, 128), 1)
    ranks = []
    for m, x in enumerate(blocks):
        same = jnp.where((down[m] == x) & earlier, 1.0, 0.0)
        for k in range(m):
            same += jnp.where(down[k] == x, 1.0, 0.0)
        ranks.append(jnp.sum(same, axis=0, keepdims=True))
    return blocks, ranks


def water_kernel(
    own, mate, edge_a, edge_b, weight, bias, level_out, ratio_out, place_out, level, row, col, bed, wet, mask, *, rows, tiles, capacity
):
    odd = lax.axis_index("terrain") % 2 == 1
    for place, target in enumerate((level, bed, wet)):
        mine = own[place * rows : (place + 1) * rows]
        other = mate[place * rows : (place + 1) * rows]
        a = edge_a[place * HALO : (place + 1) * HALO]
        b = edge_b[place * HALO : (place + 1) * HALO]
        pick = [
            jnp.where(odd, b, a),
            jnp.where(odd, other, mine),
            jnp.where(odd, mine, other),
            jnp.where(odd, a, b),
        ]
        whole = jnp.concatenate(pick, axis=0)
        if target is wet:
            whole = whole.astype(jnp.int32)
        if target is bed:
            mask[...] = (whole > 0.0).astype(f32)
        target[...] = whole
    row[...] = jnp.zeros_like(row)
    col[...] = jnp.zeros_like(col)

    mine, other = own[3 * rows : 3 * rows + 1, :tiles], mate[3 * rows : 3 * rows + 1, :tiles]
    for strip, owner in enumerate((jnp.where(odd, other, mine), jnp.where(odd, mine, other))):
        for k, (block, rank) in enumerate(zip(*ranks_of(owner))):
            record = block * (2.0 * capacity) + rank + float(strip * capacity)
            at = strip * (tiles // 128) + k
            place_out[at : at + 1] = record.astype(jnp.int32)

    def substep(step, _):
        l, r, c, d = level[...], row[...], col[...], bed[...]
        factor = (lax.shift_right_logical(wet[...], step) & 1).astype(f32)
        rf, cf = d * r, d * c
        level[...] = 0.25 * (shifted_rows(l - rf, l + rf) + shifted_columns(l - cf, l + cf)) * mask[...]
        row[...] = 0.25 * (shifted_rows(r - l, r + l) + shifted_columns(r, r)) * factor
        col[...] = 0.25 * (shifted_rows(c, c) + shifted_columns(c - l, c + l)) * factor
        return 0

    lax.fori_loop(0, SUBSTEPS, substep, 0)
    level_out[...] = jnp.where(odd, level[HALO + rows : HALO + 2 * rows], level[HALO : HALO + rows])
    pieces = level[HALO : HALO + 2 * rows].astype(bf16)
    cells = weight.shape[0]
    w = weight[...]
    half = w.shape[1] // 2
    for j in range(pieces.shape[1] // cells):
        z = jnp.dot(pieces[:, j * cells : (j + 1) * cells], w, preferred_element_type=f32) + bias[...]
        ratio = jax.nn.sigmoid(z).astype(bf16).astype(f32)
        span = slice(j * 2 * rows, (j + 1) * 2 * rows)
        ratio_out[0, span] = ratio[:, :half]
        ratio_out[1, span] = ratio[:, half:]


def gross_kernel(place, records, ratio, out, rows, bins, bins_t, *, group, per_row, tiles):
    odd = lax.axis_index("terrain") % 2
    senders, triple, cells = records.shape
    each = triple // 3

    def unpack(sender, _):
        block = records[sender].astype(jnp.int32)
        account = block[:each]
        number = jnp.where(
            ((account >> 4) & 1) == odd, ((account >> 5) << 4) | (account & 15), 4095
        )
        low = jnp.where(number < 256, number, -1)
        high = jnp.where((number >= 256) & (number < 512), number - 256, -1)
        span = pl.ds(pl.multiple_of(sender * each, each), each)
        rows[0, span] = low.astype(f32)
        rows[1, span] = high.astype(f32)
        rows[2, span] = block[2 * each :].astype(f32) * (1 / 128)
        rows[3, span] = block[each : 2 * each].astype(f32)
        return 0

    lax.fori_loop(0, senders, unpack, 0)
    strip_rows = tiles // (2 * per_row)
    per_col = 2 * strip_rows // 8

    row_bits, tile_bits, strip_bits = [x.bit_length() - 1 for x in (per_row, tiles // 2, per_col)]

    def records_of(eight):
        column, part = lax.shift_right_logical(eight, strip_bits), eight & (per_col - 1)
        strip, part = lax.shift_right_logical(part, strip_bits - 1), part & (per_col // 2 - 1)
        first = (strip << tile_bits) + (part << (row_bits + 3)) + column
        at, lane = lax.shift_right_logical(first, 7), first & 127
        return [place[at, lane + u * per_row] for u in range(8)]

    def gather(eight, _):
        for u, record in enumerate(records_of(eight)):
            bins[pl.ds(eight * 8 + u, 1), :] = rows[3, pl.ds(record, 1), :]
        return 0

    lax.fori_loop(0, tiles // 8, gather, 0)
    for k in range(tiles // 128):
        bins_t[k] = bins[k * 128 : (k + 1) * 128, :].T
    out[...] = jnp.zeros_like(out)
    number = lax.broadcasted_iota(jnp.int32, (256, cells), 0).astype(f32).astype(bf16)
    first_bins = lax.broadcasted_iota(jnp.int32, (cells, 128), 1).astype(f32).astype(bf16)
    last_bins = (lax.broadcasted_iota(jnp.int32, (cells, 128), 1) + 128).astype(f32).astype(bf16)
    no_left = jnp.zeros((256, cells), bf16)
    no_right = jnp.zeros((cells, 128), bf16)

    def spread(row, count):
        packed = jnp.broadcast_to(row, (16, 128)).astype(bf16)
        return jnp.concatenate([packed] * (count // 16), axis=0)

    def add(block, _):
        lefts, rights = [], []
        for x in range(group // 8):
            eight = block * (group // 8) + x
            shown = pltpu.roll(bins_t[lax.shift_right_logical(eight, 4)], (128 - 8 * (eight & 15)) & 127, axis=1)
            for u, record in enumerate(records_of(eight)):
                low, high, value = [spread(rows[k, pl.ds(record, 1), :], 256) for k in range(3)]
                lefts.append(
                    jnp.concatenate(
                        [jnp.where(low == number, value, no_left), jnp.where(high == number, value, no_left)],
                        axis=0,
                    )
                )
                bin_of = jnp.broadcast_to(shown[:, u : u + 1], (cells, 128)).astype(bf16)
                some = [spread(ratio[k, pl.ds(eight * 8 + u, 1), :], cells) for k in range(2)]
                rights.append(
                    jnp.concatenate(
                        [
                            jnp.where(first_bins >= bin_of, some[0], no_right),
                            jnp.where(last_bins >= bin_of, some[1], no_right),
                        ],
                        axis=1,
                    )
                )
        out[...] += jnp.dot(
            jnp.concatenate(lefts, axis=1), jnp.concatenate(rights, axis=0), preferred_element_type=f32
        )
        return 0

    lax.fori_loop(0, tiles // group, add, 0)


def per_device(
    level_start,
    bed_depth,
    wet_bits,
    tile_owner,
    vuln_weight,
    vuln_bias,
    account_index,
    bin_index,
    exposure_value,
    deductible,
    limit,
):
    _, rows, width = level_start.shape
    cells, bin_count = vuln_weight.shape
    account_count = deductible.shape[0]
    owners = lax.axis_size("terrain")
    events = lax.axis_size("event")
    me = lax.axis_index("terrain")
    slots = account_index.shape[0]
    capacity = slots // owners
    tiles = tile_owner.shape[0]
    vmem = pl.BlockSpec(memory_space=pltpu.VMEM)

    ready, own, edge = pl.pallas_call(
        functools.partial(pack_kernel, each=2 * capacity),
        in_specs=[pl.BlockSpec(memory_space=pltpu.HBM)] * 7,
        out_specs=(vmem,) * 3,
        scratch_shapes=[
            pltpu.VMEM((slots, cells), jnp.int32),
            pltpu.VMEM((slots, cells), jnp.int32),
            pltpu.VMEM((slots, cells), bf16),
            pltpu.VMEM((rows, width), f32),
            pltpu.VMEM((rows, width), f32),
            pltpu.VMEM((rows, width), jnp.int32),
            pltpu.VMEM((1, tiles), jnp.int32),
            pltpu.SemaphoreType.DMA((7,)),
        ],
        out_shape=(
            jax.ShapeDtypeStruct((owners, 6 * capacity, cells), jnp.int16),
            jax.ShapeDtypeStruct((3 * rows + 8, width), f32),
            jax.ShapeDtypeStruct((3 * HALO, width), f32),
        ),
        compiler_params=pltpu.CompilerParams(vmem_limit_bytes=60 << 20),
        name="pack",
    )(
        account_index,
        bin_index,
        exposure_value,
        level_start[0],
        bed_depth,
        wet_bits[0],
        tile_owner.reshape(1, tiles),
    )
    records = lax.all_to_all(ready, "terrain", 0, 0, tiled=True)
    mate = lax.ppermute(own, "terrain", [(i, i ^ 1) for i in range(owners)])

    def outward(step):
        pairs = [(i, i + step if i % 2 else i - step) for i in range(owners)]
        return [(i, k) for i, k in pairs if 0 <= k < owners]

    edge_a = lax.ppermute(edge, "terrain", outward(1))
    edge_b = lax.ppermute(edge, "terrain", outward(2))

    wide = (2 * (rows + HALO), width)
    level, ratio, place = pl.pallas_call(
        functools.partial(water_kernel, rows=rows, tiles=tiles, capacity=capacity),
        in_specs=[vmem] * 6,
        out_specs=(vmem,) * 3,
        out_shape=(
            jax.ShapeDtypeStruct((rows, width), f32),
            jax.ShapeDtypeStruct((2, 2 * tiles, bin_count // 2), f32),
            jax.ShapeDtypeStruct((2 * tiles // 128, 128), jnp.int32),
        ),
        scratch_shapes=[pltpu.VMEM(wide, f32)] * 4 + [pltpu.VMEM(wide, jnp.int32), pltpu.VMEM(wide, f32)],
        compiler_params=pltpu.CompilerParams(vmem_limit_bytes=32 << 20),
        cost_estimate=pl.CostEstimate(flops=1, bytes_accessed=1, transcendentals=0),
        name="water",
    )(own, mate, edge_a, edge_b, vuln_weight, vuln_bias[None])

    group = 128
    share = account_count // owners
    half_share = share // 2
    gross = pl.pallas_call(
        functools.partial(gross_kernel, group=group, per_row=width // cells, tiles=2 * tiles),
        grid_spec=pltpu.PrefetchScalarGridSpec(
            num_scalar_prefetch=1,
            grid=(),
            in_specs=[vmem, vmem],
            out_specs=vmem,
            scratch_shapes=[
                pltpu.VMEM((4, owners * 2 * capacity, cells), f32),
                pltpu.VMEM((2 * tiles, cells), f32),
                pltpu.VMEM((2 * tiles // 128, cells, 128), f32),
            ],
        ),
        out_shape=jax.ShapeDtypeStruct((account_count // 2, bin_count), f32),
        compiler_params=pltpu.CompilerParams(vmem_limit_bytes=40 << 20),
        name="gross",
    )(place, records, ratio)

    parts = lax.all_to_all(gross.reshape(owners, half_share, bin_count), "terrain", 0, 0, tiled=True)
    own_gross = parts.reshape(owners // 2, 2, half_share, bin_count).sum(axis=0).reshape(share, bin_count)
    scale = account_count / (rows * owners * width)
    own_deduct = lax.dynamic_slice_in_dim(deductible, me * share, share, 0)
    own_limit = lax.dynamic_slice_in_dim(limit, me * share, share, 0)
    net = jnp.minimum(jnp.maximum(own_gross * scale - own_deduct[:, None], 0.0), own_limit[:, None])
    everyone = jnp.broadcast_to(net.astype(bf16)[None], (owners, share, bin_count))
    net_loss = lax.all_to_all(everyone, "terrain", 0, 0, tiled=True).reshape(1, account_count, bin_count)
    others = [
        lax.ppermute(net, "event", [(i, (i + k) % events) for i in range(events)])
        for k in range(1, events)
    ]
    portfolio = sum(others, net) / events
    return (level[None], net_loss, portfolio)


def solution(mesh):
    placed = (
        P("event", "terrain", None),
        P("terrain", None),
        P("event", "terrain", None),
        P("terrain", None),
        P(),
        P(),
        P("terrain", None),
        P("terrain", None),
        P("terrain", None),
        P(),
        P(),
    )
    return jax.shard_map(
        per_device,
        mesh=mesh,
        in_specs=placed,
        out_specs=(P("event", "terrain", None), P("event", None, None), P("terrain", None)),
        check_vma=False,
    )
```

```python
import functools

import jax
import jax.numpy as jnp
from jax import lax
from jax.experimental import pallas as pl
from jax.experimental.pallas import tpu as pltpu
from jax.sharding import PartitionSpec as P

SUBSTEPS = 8
HALO = 8
f32 = jnp.float32
bf16 = jnp.bfloat16


def pack_kernel(*refs, each):
    sources, (records, own, edge), held, arrived = refs[:7], refs[7:10], refs[10:17], refs[17]
    copies = [pltpu.make_async_copy(x, y, arrived.at[k]) for k, (x, y) in enumerate(zip(sources, held))]
    for copy in copies:
        copy.start()
    account, bins, value, level, bed, wet, owner = held
    odd = lax.axis_index("terrain") % 2 == 1
    for copy in copies[:3]:
        copy.wait()

    def two_pairs(two, _):
        span = pl.ds(pl.multiple_of(two * 2 * each, 2 * each), 2 * each)
        parts = (account[span], bins[span], (value[span].astype(f32) * 128.0).astype(jnp.int32))
        for k, part in enumerate(parts):
            for pair in range(2):
                block = part[pair * each : (pair + 1) * each].astype(jnp.int16)
                for core in range(2):
                    records[two * 4 + pair * 2 + core, k * each : (k + 1) * each] = block
        return 0

    lax.fori_loop(0, records.shape[0] // 4, two_pairs, 0)
    for copy in copies[3:]:
        copy.wait()
    rows = level.shape[0]
    for k, field in enumerate((level[...], bed[...], wet[...].astype(f32))):
        own[k * rows : (k + 1) * rows] = field
        edge[k * HALO : (k + 1) * HALO] = jnp.where(odd, field[rows - HALO :], field[:HALO])
    own[3 * rows :] = jnp.zeros((own.shape[0] - 3 * rows, own.shape[1]), f32)
    own[3 * rows : 3 * rows + 1, : owner.shape[1]] = owner[...].astype(f32)


def ranks_of(owner):
    blocks = [owner[:, k : k + 128] for k in range(0, owner.shape[1], 128)]
    down = [jnp.broadcast_to(x, (128, 128)).T for x in blocks]
    earlier = lax.broadcasted_iota(jnp.int32, (128, 128), 0) < lax.broadcasted_iota(jnp.int32, (128, 128), 1)
    ranks = []
    for m, x in enumerate(blocks):
        same = jnp.where((down[m] == x) & earlier, 1.0, 0.0)
        for k in range(m):
            same += jnp.where(down[k] == x, 1.0, 0.0)
        ranks.append(jnp.sum(same, axis=0, keepdims=True))
    return blocks, ranks


def place_kernel(own, mate, place, *, row, tiles, capacity):
    odd = lax.axis_index("terrain") % 2 == 1
    mine, other = own[row : row + 1, :tiles], mate[row : row + 1, :tiles]
    for half, owner in enumerate((jnp.where(odd, other, mine), jnp.where(odd, mine, other))):
        for k, (block, rank) in enumerate(zip(*ranks_of(owner))):
            record = block * (2.0 * capacity) + rank + float(half * capacity)
            at = half * (tiles // 128) + k
            place[at : at + 1] = record.astype(jnp.int32)


def water_kernel(
    own, mate, edge_a, edge_b, weight, bias, place, level_out, ratio_out, first, second, bed, wet, *, rows
):
    del place
    odd = lax.axis_index("terrain") % 2 == 1
    columns = bed.shape[0]
    strip = rows // 8
    groups = 2 * strip + 2
    empty = jnp.zeros((columns, 8, 128), f32)
    for buffer in (first.at[0], first.at[1], first.at[2], second.at[0], second.at[1], second.at[2], bed):
        buffer[:, :8] = empty
        buffer[:, (groups + 1) * 8 :] = empty
    for g in range(groups):
        for part, target in enumerate((first.at[0], bed, wet)):
            if g in (0, groups - 1):
                span = slice(part * HALO, (part + 1) * HALO)
                even_one, odd_one = (edge_a, edge_b) if g == 0 else (edge_b, edge_a)
            else:
                at = part * rows + (g - 1) % strip * 8
                span = slice(at, at + 8)
                even_one, odd_one = (own, mate) if g <= strip else (mate, own)
            for j in range(columns):
                lanes = slice(j * 128, (j + 1) * 128)
                block = jnp.where(odd, odd_one[span, lanes], even_one[span, lanes])
                if target is wet:
                    block = block.astype(jnp.int32)
                target[j, (g + 1) * 8 : (g + 2) * 8] = block
        for k in (1, 2):
            first[k, :, (g + 1) * 8 : (g + 2) * 8] = empty

    lane = lax.broadcasted_iota(jnp.int32, (8, 128), 1)
    nothing = [jnp.zeros((8, 128), f32)] * 6

    def substep(old, new, step):
        bit = lax.shift_left(1, step)

        def turned(j, at):
            l, r, c = [old[k, j, at : at + 8] for k in range(3)]
            flow = bed[j, at : at + 8] * c
            ahead = [pltpu.roll(x, 127, axis=1) for x in (l - flow, r, c - l)]
            behind = [pltpu.roll(x, 1, axis=1) for x in (l + flow, r, c + l)]
            return ahead + behind

        for g in range(groups):
            at = (g + 1) * 8
            below, above = slice(at + 1, at + 9), slice(at - 1, at + 7)
            last, here = nothing, turned(0, at)
            for j in range(columns):
                after = turned(j + 1, at) if j + 1 < columns else nothing
                l_side, r_side, c_side = [
                    jnp.where(lane == 127, after[k], here[k]) + jnp.where(lane == 0, last[k + 3], here[k + 3])
                    for k in range(3)
                ]
                lb, rb, cb = [old[k, j, below] for k in range(3)]
                la, ra, ca = [old[k, j, above] for k in range(3)]
                l_new = 0.25 * (((lb - bed[j, below] * rb) + (la + bed[j, above] * ra)) + l_side)
                if g in (0, groups - 1):
                    l_new = jnp.where(bed[j, at : at + 8] > 0.0, l_new, 0.0)
                factor = jnp.where((wet[j, at : at + 8] & bit) != 0, 0.25, 0.0)
                new[0, j, at : at + 8] = l_new
                new[1, j, at : at + 8] = factor * (((rb - lb) + (ra + la)) + r_side)
                new[2, j, at : at + 8] = factor * ((cb + ca) + c_side)
                last, here = here, after

    def two_substeps(two, _):
        substep(first, second, 2 * two)
        substep(second, first, 2 * two + 1)
        return 0

    lax.fori_loop(0, SUBSTEPS // 2, two_substeps, 0)
    w = weight[...]
    half = w.shape[1] // 2
    for j in range(columns):
        lanes = slice(j * 128, (j + 1) * 128)
        level_out[:, lanes] = jnp.where(odd, first[0, j, 16 + rows : 16 + 2 * rows], first[0, j, 16 : 16 + rows])
        pieces = first[0, j, 16 : 16 + 2 * rows].astype(bf16)
        z = jnp.dot(pieces, w, preferred_element_type=f32) + bias[...]
        ratio = jax.nn.sigmoid(z).astype(bf16).astype(f32)
        span = slice(j * 2 * rows, (j + 1) * 2 * rows)
        ratio_out[0, span] = ratio[:, :half]
        ratio_out[1, span] = ratio[:, half:]


def gross_kernel(place, records, ratio, out, rows, bins, bins_t, *, group, per_row, tiles):
    odd = lax.axis_index("terrain") % 2
    senders, triple, cells = records.shape
    each = triple // 3

    def unpack(sender, _):
        block = records[sender].astype(jnp.int32)
        account = block[:each]
        number = jnp.where(
            ((account >> 5) & 1) == odd, ((account >> 6) << 5) | (account & 31), 4095
        )
        low = jnp.where(number < 256, number, -1)
        high = jnp.where((number >= 256) & (number < 512), number - 256, -1)
        span = pl.ds(pl.multiple_of(sender * each, each), each)
        rows[0, span] = low.astype(f32)
        rows[1, span] = high.astype(f32)
        rows[2, span] = block[2 * each :].astype(f32) * (1 / 128)
        rows[3, span] = block[each : 2 * each].astype(f32)
        return 0

    lax.fori_loop(0, senders, unpack, 0)
    strip_rows = tiles // (2 * per_row)
    per_col = 2 * strip_rows // 8

    row_bits, tile_bits, strip_bits = [x.bit_length() - 1 for x in (per_row, tiles // 2, per_col)]

    def records_of(eight):
        column, part = lax.shift_right_logical(eight, strip_bits), eight & (per_col - 1)
        strip, part = lax.shift_right_logical(part, strip_bits - 1), part & (per_col // 2 - 1)
        first = (strip << tile_bits) + (part << (row_bits + 3)) + column
        at, lane = lax.shift_right_logical(first, 7), first & 127
        return [place[at, lane + u * per_row] for u in range(8)]

    def gather(eight, _):
        for u, record in enumerate(records_of(eight)):
            bins[pl.ds(eight * 8 + u, 1), :] = rows[3, pl.ds(record, 1), :]
        return 0

    lax.fori_loop(0, tiles // 8, gather, 0)
    for k in range(tiles // 128):
        bins_t[k] = bins[k * 128 : (k + 1) * 128, :].T
    out[...] = jnp.zeros_like(out)
    number = lax.broadcasted_iota(jnp.int32, (256, cells), 0).astype(f32).astype(bf16)
    first_bins = lax.broadcasted_iota(jnp.int32, (cells, 128), 1).astype(f32).astype(bf16)
    last_bins = (lax.broadcasted_iota(jnp.int32, (cells, 128), 1) + 128).astype(f32).astype(bf16)
    no_left = jnp.zeros((256, cells), bf16)
    no_right = jnp.zeros((cells, 128), bf16)

    def spread(row, count):
        packed = jnp.broadcast_to(row, (16, 128)).astype(bf16)
        return jnp.concatenate([packed] * (count // 16), axis=0)

    def add(block, _):
        lefts, rights = [], []
        for x in range(group // 8):
            eight = block * (group // 8) + x
            shown = pltpu.roll(bins_t[lax.shift_right_logical(eight, 4)], (128 - 8 * (eight & 15)) & 127, axis=1)
            for u, record in enumerate(records_of(eight)):
                low, high, value = [spread(rows[k, pl.ds(record, 1), :], 256) for k in range(3)]
                lefts.append(
                    jnp.concatenate(
                        [jnp.where(low == number, value, no_left), jnp.where(high == number, value, no_left)],
                        axis=0,
                    )
                )
                bin_of = jnp.broadcast_to(shown[:, u : u + 1], (cells, 128)).astype(bf16)
                some = [spread(ratio[k, pl.ds(eight * 8 + u, 1), :], cells) for k in range(2)]
                rights.append(
                    jnp.concatenate(
                        [
                            jnp.where(first_bins >= bin_of, some[0], no_right),
                            jnp.where(last_bins >= bin_of, some[1], no_right),
                        ],
                        axis=1,
                    )
                )
        out[...] += jnp.dot(
            jnp.concatenate(lefts, axis=1), jnp.concatenate(rights, axis=0), preferred_element_type=f32
        )
        return 0

    lax.fori_loop(0, tiles // group, add, 0)


def per_device(
    level_start,
    bed_depth,
    wet_bits,
    tile_owner,
    vuln_weight,
    vuln_bias,
    account_index,
    bin_index,
    exposure_value,
    deductible,
    limit,
):
    _, rows, width = level_start.shape
    cells, bin_count = vuln_weight.shape
    account_count = deductible.shape[0]
    owners = lax.axis_size("terrain")
    events = lax.axis_size("event")
    me = lax.axis_index("terrain")
    slots = account_index.shape[0]
    capacity = slots // owners
    tiles = tile_owner.shape[0]
    vmem = pl.BlockSpec(memory_space=pltpu.VMEM)

    ready, own, edge = pl.pallas_call(
        functools.partial(pack_kernel, each=2 * capacity),
        in_specs=[pl.BlockSpec(memory_space=pltpu.HBM)] * 7,
        out_specs=(vmem,) * 3,
        scratch_shapes=[
            pltpu.VMEM((slots, cells), jnp.int32),
            pltpu.VMEM((slots, cells), jnp.int32),
            pltpu.VMEM((slots, cells), bf16),
            pltpu.VMEM((rows, width), f32),
            pltpu.VMEM((rows, width), f32),
            pltpu.VMEM((rows, width), jnp.int32),
            pltpu.VMEM((1, tiles), jnp.int32),
            pltpu.SemaphoreType.DMA((7,)),
        ],
        out_shape=(
            jax.ShapeDtypeStruct((owners, 6 * capacity, cells), jnp.int16),
            jax.ShapeDtypeStruct((3 * rows + 8, width), f32),
            jax.ShapeDtypeStruct((3 * HALO, width), f32),
        ),
        compiler_params=pltpu.CompilerParams(vmem_limit_bytes=60 << 20),
        name="pack",
    )(
        account_index,
        bin_index,
        exposure_value,
        level_start[0],
        bed_depth,
        wet_bits[0],
        tile_owner.reshape(1, tiles),
    )
    records = lax.all_to_all(ready, "terrain", 0, 0, tiled=True)
    mate = lax.ppermute(own, "terrain", [(i, i ^ 1) for i in range(owners)])

    def outward(step):
        pairs = [(i, i + step if i % 2 else i - step) for i in range(owners)]
        return [(i, k) for i, k in pairs if 0 <= k < owners]

    edge_a = lax.ppermute(edge, "terrain", outward(1))
    edge_b = lax.ppermute(edge, "terrain", outward(2))

    held = (width // 128, 2 * (rows + HALO) + 16, 128)
    place = pl.pallas_call(
        functools.partial(place_kernel, row=0, tiles=tiles, capacity=capacity),
        in_specs=[vmem] * 2,
        out_specs=vmem,
        out_shape=jax.ShapeDtypeStruct((2 * tiles // 128, 128), jnp.int32),
        compiler_params=pltpu.CompilerParams(vmem_limit_bytes=16 << 20),
        cost_estimate=pl.CostEstimate(flops=10_000_000, bytes_accessed=4_000_000, transcendentals=0),
        name="place",
    )(own[3 * rows :], mate[3 * rows :])
    level, ratio = pl.pallas_call(
        functools.partial(water_kernel, rows=rows),
        in_specs=[vmem] * 7,
        out_specs=(vmem,) * 2,
        out_shape=(
            jax.ShapeDtypeStruct((rows, width), f32),
            jax.ShapeDtypeStruct((2, 2 * tiles, bin_count // 2), f32),
        ),
        scratch_shapes=[
            pltpu.VMEM((3, *held), f32),
            pltpu.VMEM((3, *held), f32),
            pltpu.VMEM(held, f32),
            pltpu.VMEM(held, jnp.int32),
        ],
        compiler_params=pltpu.CompilerParams(vmem_limit_bytes=32 << 20),
        cost_estimate=pl.CostEstimate(flops=1, bytes_accessed=1, transcendentals=0),
        name="water",
    )(own, mate, edge_a, edge_b, vuln_weight, vuln_bias[None], place)

    group = 128
    share = account_count // owners
    gross = pl.pallas_call(
        functools.partial(gross_kernel, group=group, per_row=width // cells, tiles=2 * tiles),
        grid_spec=pltpu.PrefetchScalarGridSpec(
            num_scalar_prefetch=1,
            grid=(),
            in_specs=[vmem, vmem],
            out_specs=vmem,
            scratch_shapes=[
                pltpu.VMEM((4, owners * 2 * capacity, cells), f32),
                pltpu.VMEM((2 * tiles, cells), f32),
                pltpu.VMEM((2 * tiles // 128, cells, 128), f32),
            ],
        ),
        out_shape=jax.ShapeDtypeStruct((account_count // 2, bin_count), f32),
        compiler_params=pltpu.CompilerParams(vmem_limit_bytes=40 << 20),
        name="gross",
    )(place, records, ratio)

    alike = [list(range(core, owners, 2)) for core in range(2)]
    parts = lax.all_to_all(
        gross.reshape(owners // 2, share, bin_count), "terrain", 0, 0, tiled=True, axis_index_groups=alike
    )
    own_gross = parts.sum(axis=0)
    scale = account_count / (rows * owners * width)
    own_deduct = lax.dynamic_slice_in_dim(deductible, me * share, share, 0)
    own_limit = lax.dynamic_slice_in_dim(limit, me * share, share, 0)
    net = jnp.minimum(jnp.maximum(own_gross * scale - own_deduct[:, None], 0.0), own_limit[:, None])
    everyone = jnp.broadcast_to(net.astype(bf16)[None], (owners, share, bin_count))
    net_loss = lax.all_to_all(everyone, "terrain", 0, 0, tiled=True).reshape(1, account_count, bin_count)
    others = [
        lax.ppermute(net, "event", [(i, (i + k) % events) for i in range(events)])
        for k in range(1, events)
    ]
    portfolio = sum(others, net) / events
    return (level[None], net_loss, portfolio)


def solution(mesh):
    placed = (
        P("event", "terrain", None),
        P("terrain", None),
        P("event", "terrain", None),
        P("terrain", None),
        P(),
        P(),
        P("terrain", None),
        P("terrain", None),
        P("terrain", None),
        P(),
        P(),
    )
    return jax.shard_map(
        per_device,
        mesh=mesh,
        in_specs=placed,
        out_specs=(P("event", "terrain", None), P("event", None, None), P("terrain", None)),
        check_vma=False,
    )
```

```python
import functools

import jax
import jax.numpy as jnp
from jax import lax
from jax.experimental import pallas as pl
from jax.experimental.pallas import tpu as pltpu
from jax.sharding import PartitionSpec as P

SUBSTEPS = 8
HALO = 8
f32 = jnp.float32
bf16 = jnp.bfloat16


def pack_kernel(*refs, each):
    sources, (records, own, edge), held, arrived = refs[:7], refs[7:10], refs[10:17], refs[17]
    copies = [pltpu.make_async_copy(x, y, arrived.at[k]) for k, (x, y) in enumerate(zip(sources, held))]
    for copy in copies:
        copy.start()
    account, bins, value, level, bed, wet, owner = held
    odd = lax.axis_index("terrain") % 2 == 1
    for copy in copies[:3]:
        copy.wait()

    def two_pairs(two, _):
        span = pl.ds(pl.multiple_of(two * 2 * each, 2 * each), 2 * each)
        parts = (account[span], bins[span], (value[span].astype(f32) * 128.0).astype(jnp.int32))
        for k, part in enumerate(parts):
            for pair in range(2):
                block = part[pair * each : (pair + 1) * each].astype(jnp.int16)
                for core in range(2):
                    records[two * 4 + pair * 2 + core, k * each : (k + 1) * each] = block
        return 0

    lax.fori_loop(0, records.shape[0] // 4, two_pairs, 0, unroll=True)
    for copy in copies[3:]:
        copy.wait()
    rows = level.shape[0]
    for k, field in enumerate((level[...], bed[...], wet[...].astype(f32))):
        own[k * rows : (k + 1) * rows] = field
        edge[k * HALO : (k + 1) * HALO] = jnp.where(odd, field[rows - HALO :], field[:HALO])
    own[3 * rows :] = jnp.zeros((own.shape[0] - 3 * rows, own.shape[1]), f32)
    own[3 * rows : 3 * rows + 1, : owner.shape[1]] = owner[...].astype(f32)


def ranks_of(owner):
    blocks = [owner[:, k : k + 128] for k in range(0, owner.shape[1], 128)]
    down = [jnp.broadcast_to(x, (128, 128)).T for x in blocks]
    earlier = lax.broadcasted_iota(jnp.int32, (128, 128), 0) < lax.broadcasted_iota(jnp.int32, (128, 128), 1)
    ranks = []
    for m, x in enumerate(blocks):
        same = jnp.where((down[m] == x) & earlier, 1.0, 0.0)
        for k in range(m):
            same += jnp.where(down[k] == x, 1.0, 0.0)
        ranks.append(jnp.sum(same, axis=0, keepdims=True))
    return blocks, ranks


def place_kernel(own, mate, place, *, row, tiles, capacity):
    odd = lax.axis_index("terrain") % 2 == 1
    mine, other = own[row : row + 1, :tiles], mate[row : row + 1, :tiles]
    for half, owner in enumerate((jnp.where(odd, other, mine), jnp.where(odd, mine, other))):
        for k, (block, rank) in enumerate(zip(*ranks_of(owner))):
            record = block * (2.0 * capacity) + rank + float(half * capacity)
            at = half * (tiles // 128) + k
            place[at : at + 1] = record.astype(jnp.int32)


def water_kernel(
    own, mate, edge_a, edge_b, weight, bias, place, level_out, ratio_out, first, second, bed, wet, *, rows
):
    del place
    odd = lax.axis_index("terrain") % 2 == 1
    columns = bed.shape[0]
    strip = rows // 8
    groups = 2 * strip + 2
    empty = jnp.zeros((columns, 8, 128), f32)
    for buffer in (first.at[0], first.at[1], first.at[2], second.at[0], second.at[1], second.at[2], bed):
        buffer[:, :8] = empty
        buffer[:, (groups + 1) * 8 :] = empty
    for g in range(groups):
        for part, target in enumerate((first.at[0], bed, wet)):
            if g in (0, groups - 1):
                span = slice(part * HALO, (part + 1) * HALO)
                even_one, odd_one = (edge_a, edge_b) if g == 0 else (edge_b, edge_a)
            else:
                at = part * rows + (g - 1) % strip * 8
                span = slice(at, at + 8)
                even_one, odd_one = (own, mate) if g <= strip else (mate, own)
            for j in range(columns):
                lanes = slice(j * 128, (j + 1) * 128)
                block = jnp.where(odd, odd_one[span, lanes], even_one[span, lanes])
                if target is wet:
                    block = block.astype(jnp.int32)
                target[j, (g + 1) * 8 : (g + 2) * 8] = block
        for k in (1, 2):
            first[k, :, (g + 1) * 8 : (g + 2) * 8] = empty

    lane = lax.broadcasted_iota(jnp.int32, (8, 128), 1)
    nothing = [jnp.zeros((8, 128), f32)] * 6

    def substep(old, new, step):
        bit = lax.shift_left(1, step)

        def turned(j, at):
            l, r, c = [old[k, j, at : at + 8] for k in range(3)]
            flow = bed[j, at : at + 8] * c
            ahead = [pltpu.roll(x, 127, axis=1) for x in (l - flow, r, c - l)]
            behind = [pltpu.roll(x, 1, axis=1) for x in (l + flow, r, c + l)]
            return ahead + behind

        for g in range(groups):
            at = (g + 1) * 8
            below, above = slice(at + 1, at + 9), slice(at - 1, at + 7)
            last, here = nothing, turned(0, at)
            for j in range(columns):
                after = turned(j + 1, at) if j + 1 < columns else nothing
                l_side, r_side, c_side = [
                    jnp.where(lane == 127, after[k], here[k]) + jnp.where(lane == 0, last[k + 3], here[k + 3])
                    for k in range(3)
                ]
                lb, rb, cb = [old[k, j, below] for k in range(3)]
                la, ra, ca = [old[k, j, above] for k in range(3)]
                l_new = 0.25 * (((lb - bed[j, below] * rb) + (la + bed[j, above] * ra)) + l_side)
                if g in (0, groups - 1):
                    l_new = jnp.where(bed[j, at : at + 8] > 0.0, l_new, 0.0)
                factor = jnp.where((wet[j, at : at + 8] & bit) != 0, 0.25, 0.0)
                new[0, j, at : at + 8] = l_new
                new[1, j, at : at + 8] = factor * (((rb - lb) + (ra + la)) + r_side)
                new[2, j, at : at + 8] = factor * ((cb + ca) + c_side)
                last, here = here, after

    def two_substeps(two, _):
        substep(first, second, 2 * two)
        substep(second, first, 2 * two + 1)
        return 0

    lax.fori_loop(0, SUBSTEPS // 2, two_substeps, 0)
    w = weight[...]
    half = w.shape[1] // 2
    for j in range(columns):
        lanes = slice(j * 128, (j + 1) * 128)
        level_out[:, lanes] = jnp.where(odd, first[0, j, 16 + rows : 16 + 2 * rows], first[0, j, 16 : 16 + rows])
        pieces = first[0, j, 16 : 16 + 2 * rows].astype(bf16)
        z = jnp.dot(pieces, w, preferred_element_type=f32) + bias[...]
        ratio = jax.nn.sigmoid(z).astype(bf16).astype(f32)
        span = slice(j * 2 * rows, (j + 1) * 2 * rows)
        ratio_out[0, span] = ratio[:, :half]
        ratio_out[1, span] = ratio[:, half:]


def gross_kernel(place, records, ratio, out, rows, bins, bins_t, *, group, per_row, tiles):
    odd = lax.axis_index("terrain") % 2
    senders, triple, cells = records.shape
    each = triple // 3

    def unpack(sender, _):
        block = records[sender].astype(jnp.int32)
        account = block[:each]
        number = jnp.where(
            ((account >> 5) & 1) == odd, ((account >> 6) << 5) | (account & 31), 4095
        )
        low = jnp.where(number < 256, number, -1)
        high = jnp.where((number >= 256) & (number < 512), number - 256, -1)
        span = pl.ds(pl.multiple_of(sender * each, each), each)
        rows[0, span] = low.astype(f32)
        rows[1, span] = high.astype(f32)
        rows[2, span] = block[2 * each :].astype(f32) * (1 / 128)
        rows[3, span] = block[each : 2 * each].astype(f32)
        return 0

    lax.fori_loop(0, senders, unpack, 0, unroll=4)
    strip_rows = tiles // (2 * per_row)
    per_col = 2 * strip_rows // 8

    row_bits, tile_bits, strip_bits = [x.bit_length() - 1 for x in (per_row, tiles // 2, per_col)]

    def records_of(eight):
        column, part = lax.shift_right_logical(eight, strip_bits), eight & (per_col - 1)
        strip, part = lax.shift_right_logical(part, strip_bits - 1), part & (per_col // 2 - 1)
        first = (strip << tile_bits) + (part << (row_bits + 3)) + column
        at, lane = lax.shift_right_logical(first, 7), first & 127
        return [place[at, lane + u * per_row] for u in range(8)]

    def gather(eight, _):
        for u, record in enumerate(records_of(eight)):
            bins[pl.ds(eight * 8 + u, 1), :] = rows[3, pl.ds(record, 1), :]
        return 0

    lax.fori_loop(0, tiles // 8, gather, 0, unroll=4)
    for k in range(tiles // 128):
        bins_t[k] = bins[k * 128 : (k + 1) * 128, :].T
    out[...] = jnp.zeros_like(out)
    number = lax.broadcasted_iota(jnp.int32, (256, cells), 0).astype(f32).astype(bf16)
    first_bins = lax.broadcasted_iota(jnp.int32, (cells, 128), 1).astype(f32).astype(bf16)
    last_bins = (lax.broadcasted_iota(jnp.int32, (cells, 128), 1) + 128).astype(f32).astype(bf16)
    no_left = jnp.zeros((256, cells), bf16)
    no_right = jnp.zeros((cells, 128), bf16)

    def spread(row, count):
        packed = jnp.broadcast_to(row, (16, 128)).astype(bf16)
        return jnp.concatenate([packed] * (count // 16), axis=0)

    def add(block, _):
        lefts, rights = [], []
        for x in range(group // 8):
            eight = block * (group // 8) + x
            shown = pltpu.roll(bins_t[lax.shift_right_logical(eight, 4)], (128 - 8 * (eight & 15)) & 127, axis=1)
            for u, record in enumerate(records_of(eight)):
                low, high, value = [spread(rows[k, pl.ds(record, 1), :], 256) for k in range(3)]
                lefts.append(
                    jnp.concatenate(
                        [jnp.where(low == number, value, no_left), jnp.where(high == number, value, no_left)],
                        axis=0,
                    )
                )
                bin_of = jnp.broadcast_to(shown[:, u : u + 1], (cells, 128)).astype(bf16)
                some = [spread(ratio[k, pl.ds(eight * 8 + u, 1), :], cells) for k in range(2)]
                rights.append(
                    jnp.concatenate(
                        [
                            jnp.where(first_bins >= bin_of, some[0], no_right),
                            jnp.where(last_bins >= bin_of, some[1], no_right),
                        ],
                        axis=1,
                    )
                )
        out[...] += jnp.dot(
            jnp.concatenate(lefts, axis=1), jnp.concatenate(rights, axis=0), preferred_element_type=f32
        )
        return 0

    lax.fori_loop(0, tiles // group, add, 0)


def per_device(
    level_start,
    bed_depth,
    wet_bits,
    tile_owner,
    vuln_weight,
    vuln_bias,
    account_index,
    bin_index,
    exposure_value,
    deductible,
    limit,
):
    _, rows, width = level_start.shape
    cells, bin_count = vuln_weight.shape
    account_count = deductible.shape[0]
    owners = lax.axis_size("terrain")
    events = lax.axis_size("event")
    me = lax.axis_index("terrain")
    slots = account_index.shape[0]
    capacity = slots // owners
    tiles = tile_owner.shape[0]
    vmem = pl.BlockSpec(memory_space=pltpu.VMEM)

    ready, own, edge = pl.pallas_call(
        functools.partial(pack_kernel, each=2 * capacity),
        in_specs=[pl.BlockSpec(memory_space=pltpu.HBM)] * 7,
        out_specs=(vmem,) * 3,
        scratch_shapes=[
            pltpu.VMEM((slots, cells), jnp.int32),
            pltpu.VMEM((slots, cells), jnp.int32),
            pltpu.VMEM((slots, cells), bf16),
            pltpu.VMEM((rows, width), f32),
            pltpu.VMEM((rows, width), f32),
            pltpu.VMEM((rows, width), jnp.int32),
            pltpu.VMEM((1, tiles), jnp.int32),
            pltpu.SemaphoreType.DMA((7,)),
        ],
        out_shape=(
            jax.ShapeDtypeStruct((owners, 6 * capacity, cells), jnp.int16),
            jax.ShapeDtypeStruct((3 * rows + 8, width), f32),
            jax.ShapeDtypeStruct((3 * HALO, width), f32),
        ),
        compiler_params=pltpu.CompilerParams(vmem_limit_bytes=60 << 20),
        name="pack",
    )(
        account_index,
        bin_index,
        exposure_value,
        level_start[0],
        bed_depth,
        wet_bits[0],
        tile_owner.reshape(1, tiles),
    )
    records = lax.all_to_all(ready, "terrain", 0, 0, tiled=True)
    mate = lax.ppermute(own, "terrain", [(i, i ^ 1) for i in range(owners)])

    def outward(step):
        pairs = [(i, i + step if i % 2 else i - step) for i in range(owners)]
        return [(i, k) for i, k in pairs if 0 <= k < owners]

    edge_a = lax.ppermute(edge, "terrain", outward(1))
    edge_b = lax.ppermute(edge, "terrain", outward(2))

    held = (width // 128, 2 * (rows + HALO) + 16, 128)
    place = pl.pallas_call(
        functools.partial(place_kernel, row=0, tiles=tiles, capacity=capacity),
        in_specs=[vmem] * 2,
        out_specs=vmem,
        out_shape=jax.ShapeDtypeStruct((2 * tiles // 128, 128), jnp.int32),
        compiler_params=pltpu.CompilerParams(vmem_limit_bytes=16 << 20),
        cost_estimate=pl.CostEstimate(flops=10_000_000, bytes_accessed=4_000_000, transcendentals=0),
        name="place",
    )(own[3 * rows :], mate[3 * rows :])
    level, ratio = pl.pallas_call(
        functools.partial(water_kernel, rows=rows),
        in_specs=[vmem] * 7,
        out_specs=(vmem,) * 2,
        out_shape=(
            jax.ShapeDtypeStruct((rows, width), f32),
            jax.ShapeDtypeStruct((2, 2 * tiles, bin_count // 2), f32),
        ),
        scratch_shapes=[
            pltpu.VMEM((3, *held), f32),
            pltpu.VMEM((3, *held), f32),
            pltpu.VMEM(held, f32),
            pltpu.VMEM(held, jnp.int32),
        ],
        compiler_params=pltpu.CompilerParams(vmem_limit_bytes=32 << 20),
        cost_estimate=pl.CostEstimate(flops=1, bytes_accessed=1, transcendentals=0),
        name="water",
    )(own, mate, edge_a, edge_b, vuln_weight, vuln_bias[None], place)

    group = 128
    share = account_count // owners
    gross = pl.pallas_call(
        functools.partial(gross_kernel, group=group, per_row=width // cells, tiles=2 * tiles),
        grid_spec=pltpu.PrefetchScalarGridSpec(
            num_scalar_prefetch=1,
            grid=(),
            in_specs=[vmem, vmem],
            out_specs=vmem,
            scratch_shapes=[
                pltpu.VMEM((4, owners * 2 * capacity, cells), f32),
                pltpu.VMEM((2 * tiles, cells), f32),
                pltpu.VMEM((2 * tiles // 128, cells, 128), f32),
            ],
        ),
        out_shape=jax.ShapeDtypeStruct((account_count // 2, bin_count), f32),
        compiler_params=pltpu.CompilerParams(vmem_limit_bytes=40 << 20),
        name="gross",
    )(place, records, ratio)

    alike = [list(range(core, owners, 2)) for core in range(2)]
    parts = lax.all_to_all(
        gross.reshape(owners // 2, share, bin_count), "terrain", 0, 0, tiled=True, axis_index_groups=alike
    )
    own_gross = parts.sum(axis=0)
    scale = account_count / (rows * owners * width)
    own_deduct = lax.dynamic_slice_in_dim(deductible, me * share, share, 0)
    own_limit = lax.dynamic_slice_in_dim(limit, me * share, share, 0)
    net = jnp.minimum(jnp.maximum(own_gross * scale - own_deduct[:, None], 0.0), own_limit[:, None])
    everyone = jnp.broadcast_to(net.astype(bf16)[None], (owners, share, bin_count))
    net_loss = lax.all_to_all(everyone, "terrain", 0, 0, tiled=True).reshape(1, account_count, bin_count)
    others = [
        lax.ppermute(net, "event", [(i, (i + k) % events) for i in range(events)])
        for k in range(1, events)
    ]
    portfolio = sum(others, net) / events
    return (level[None], net_loss, portfolio)


def solution(mesh):
    placed = (
        P("event", "terrain", None),
        P("terrain", None),
        P("event", "terrain", None),
        P("terrain", None),
        P(),
        P(),
        P("terrain", None),
        P("terrain", None),
        P("terrain", None),
        P(),
        P(),
    )
    return jax.shard_map(
        per_device,
        mesh=mesh,
        in_specs=placed,
        out_specs=(P("event", "terrain", None), P("event", None, None), P("terrain", None)),
        check_vma=False,
    )
```

```python
import functools

import jax
import jax.numpy as jnp
from jax import lax
from jax.experimental import pallas as pl
from jax.experimental.pallas import tpu as pltpu
from jax.sharding import PartitionSpec as P

SUBSTEPS = 8
HALO = 8
f32 = jnp.float32
bf16 = jnp.bfloat16


def pack_kernel(*refs, each):
    sources, (records, own, edge), held, arrived = refs[:7], refs[7:10], refs[10:17], refs[17]
    copies = [pltpu.make_async_copy(x, y, arrived.at[k]) for k, (x, y) in enumerate(zip(sources, held))]
    for copy in copies:
        copy.start()
    account, bins, value, level, bed, wet, owner = held
    odd = lax.axis_index("terrain") % 2 == 1
    for copy in copies[:3]:
        copy.wait()

    def two_pairs(two, _):
        span = pl.ds(pl.multiple_of(two * 2 * each, 2 * each), 2 * each)
        parts = (account[span], bins[span], (value[span].astype(f32) * 128.0).astype(jnp.int32))
        for k, part in enumerate(parts):
            for pair in range(2):
                block = part[pair * each : (pair + 1) * each].astype(jnp.int16)
                for core in range(2):
                    records[two * 4 + pair * 2 + core, k * each : (k + 1) * each] = block
        return 0

    lax.fori_loop(0, records.shape[0] // 4, two_pairs, 0, unroll=True)
    for copy in copies[3:]:
        copy.wait()
    rows = level.shape[0]
    for k, field in enumerate((level[...], bed[...], wet[...].astype(f32))):
        own[k * rows : (k + 1) * rows] = field
        edge[k * HALO : (k + 1) * HALO] = jnp.where(odd, field[rows - HALO :], field[:HALO])
    own[3 * rows :] = jnp.zeros((own.shape[0] - 3 * rows, own.shape[1]), f32)
    own[3 * rows : 3 * rows + 1, : owner.shape[1]] = owner[...].astype(f32)


def ranks_of(owner):
    blocks = [owner[:, k : k + 128] for k in range(0, owner.shape[1], 128)]
    down = [jnp.broadcast_to(x, (128, 128)).T for x in blocks]
    earlier = lax.broadcasted_iota(jnp.int32, (128, 128), 0) < lax.broadcasted_iota(jnp.int32, (128, 128), 1)
    ranks = []
    for m, x in enumerate(blocks):
        same = jnp.where((down[m] == x) & earlier, 1.0, 0.0)
        for k in range(m):
            same += jnp.where(down[k] == x, 1.0, 0.0)
        ranks.append(jnp.sum(same, axis=0, keepdims=True))
    return blocks, ranks


def place_kernel(own, mate, place, *, row, tiles, capacity):
    odd = lax.axis_index("terrain") % 2 == 1
    mine, other = own[row : row + 1, :tiles], mate[row : row + 1, :tiles]
    for half, owner in enumerate((jnp.where(odd, other, mine), jnp.where(odd, mine, other))):
        for k, (block, rank) in enumerate(zip(*ranks_of(owner))):
            record = block * (2.0 * capacity) + rank + float(half * capacity)
            at = half * (tiles // 128) + k
            place[at : at + 1] = record.astype(jnp.int32)


def water_kernel(
    own, mate, edge_a, edge_b, weight, bias, place, level_out, ratio_out, first, second, bed, wet, *, rows
):
    del place
    odd = lax.axis_index("terrain") % 2 == 1
    columns = bed.shape[0]
    strip = rows // 8
    groups = 2 * strip + 2
    empty = jnp.zeros((columns, 8, 128), f32)
    for buffer in (first.at[0], first.at[1], first.at[2], second.at[0], second.at[1], second.at[2], bed):
        buffer[:, :8] = empty
        buffer[:, (groups + 1) * 8 :] = empty
    for g in range(groups):
        for part, target in enumerate((first.at[0], bed, wet)):
            if g in (0, groups - 1):
                span = slice(part * HALO, (part + 1) * HALO)
                even_one, odd_one = (edge_a, edge_b) if g == 0 else (edge_b, edge_a)
            else:
                at = part * rows + (g - 1) % strip * 8
                span = slice(at, at + 8)
                even_one, odd_one = (own, mate) if g <= strip else (mate, own)
            for j in range(columns):
                lanes = slice(j * 128, (j + 1) * 128)
                block = jnp.where(odd, odd_one[span, lanes], even_one[span, lanes])
                if target is wet:
                    block = block.astype(jnp.int32)
                target[j, (g + 1) * 8 : (g + 2) * 8] = block
        for k in (1, 2):
            first[k, :, (g + 1) * 8 : (g + 2) * 8] = empty

    lane = lax.broadcasted_iota(jnp.int32, (8, 128), 1)
    nothing = [jnp.zeros((8, 128), f32)] * 6

    def substep(old, new, step):
        bit = lax.shift_left(1, step)

        def turned(j, at):
            l, r, c = [old[k, j, at : at + 8] for k in range(3)]
            flow = bed[j, at : at + 8] * c
            ahead = [pltpu.roll(x, 127, axis=1) for x in (l - flow, r, c - l)]
            behind = [pltpu.roll(x, 1, axis=1) for x in (l + flow, r, c + l)]
            return ahead + behind

        for g in range(groups):
            at = (g + 1) * 8
            below, above = slice(at + 1, at + 9), slice(at - 1, at + 7)
            last, here = nothing, turned(0, at)
            for j in range(columns):
                after = turned(j + 1, at) if j + 1 < columns else nothing
                l_side, r_side, c_side = [
                    jnp.where(lane == 127, after[k], here[k]) + jnp.where(lane == 0, last[k + 3], here[k + 3])
                    for k in range(3)
                ]
                lb, rb, cb = [old[k, j, below] for k in range(3)]
                la, ra, ca = [old[k, j, above] for k in range(3)]
                l_new = 0.25 * (((lb - bed[j, below] * rb) + (la + bed[j, above] * ra)) + l_side)
                if g in (0, groups - 1):
                    l_new = jnp.where(bed[j, at : at + 8] > 0.0, l_new, 0.0)
                factor = jnp.where((wet[j, at : at + 8] & bit) != 0, 0.25, 0.0)
                new[0, j, at : at + 8] = l_new
                new[1, j, at : at + 8] = factor * (((rb - lb) + (ra + la)) + r_side)
                new[2, j, at : at + 8] = factor * ((cb + ca) + c_side)
                last, here = here, after

    def two_substeps(two, _):
        substep(first, second, 2 * two)
        substep(second, first, 2 * two + 1)
        return 0

    lax.fori_loop(0, SUBSTEPS // 2, two_substeps, 0)
    w = weight[...]
    half = w.shape[1] // 2
    for j in range(columns):
        lanes = slice(j * 128, (j + 1) * 128)
        level_out[:, lanes] = jnp.where(odd, first[0, j, 16 + rows : 16 + 2 * rows], first[0, j, 16 : 16 + rows])
        pieces = first[0, j, 16 : 16 + 2 * rows].astype(bf16)
        z = jnp.dot(pieces, w, preferred_element_type=f32) + bias[...]
        ratio = jax.nn.sigmoid(z).astype(bf16).astype(f32)
        span = slice(j * 2 * rows, (j + 1) * 2 * rows)
        ratio_out[0, span] = ratio[:, :half]
        ratio_out[1, span] = ratio[:, half:]


def gross_kernel(place, records, ratio, out, rows, bins, bins_t, *, group, per_row, tiles):
    odd = lax.axis_index("terrain") % 2
    senders, triple, cells = records.shape
    each = triple // 3

    def unpack(sender, _):
        block = records[sender].astype(jnp.int32)
        account = block[:each]
        number = jnp.where(
            ((account >> 5) & 1) == odd, ((account >> 6) << 5) | (account & 31), 4095
        )
        low = jnp.where(number < 256, number, -1)
        high = jnp.where((number >= 256) & (number < 512), number - 256, -1)
        span = pl.ds(pl.multiple_of(sender * each, each), each)
        rows[0, span] = low.astype(f32)
        rows[1, span] = high.astype(f32)
        rows[2, span] = block[2 * each :].astype(f32) * (1 / 128)
        rows[3, span] = block[each : 2 * each].astype(f32)
        return 0

    lax.fori_loop(0, senders, unpack, 0, unroll=4)
    strip_rows = tiles // (2 * per_row)
    per_col = 2 * strip_rows // 8

    row_bits, tile_bits, strip_bits = [x.bit_length() - 1 for x in (per_row, tiles // 2, per_col)]

    def records_of(eight):
        column, part = lax.shift_right_logical(eight, strip_bits), eight & (per_col - 1)
        strip, part = lax.shift_right_logical(part, strip_bits - 1), part & (per_col // 2 - 1)
        first = (strip << tile_bits) + (part << (row_bits + 3)) + column
        at, lane = lax.shift_right_logical(first, 7), first & 127
        return [place[at, lane + u * per_row] for u in range(8)]

    def gather(eight, _):
        for u, record in enumerate(records_of(eight)):
            bins[pl.ds(eight * 8 + u, 1), :] = rows[3, pl.ds(record, 1), :]
        return 0

    lax.fori_loop(0, tiles // 8, gather, 0, unroll=4)
    for k in range(tiles // 128):
        bins_t[k] = bins[k * 128 : (k + 1) * 128, :].T
    out[...] = jnp.zeros_like(out)
    number = lax.broadcasted_iota(jnp.int32, (256, cells), 0).astype(f32).astype(bf16)
    first_bins = lax.broadcasted_iota(jnp.int32, (cells, 128), 1).astype(f32).astype(bf16)
    last_bins = (lax.broadcasted_iota(jnp.int32, (cells, 128), 1) + 128).astype(f32).astype(bf16)
    no_left = jnp.zeros((256, cells), bf16)
    no_right = jnp.zeros((cells, 128), bf16)

    def spread(row, count):
        packed = jnp.broadcast_to(row, (16, 128)).astype(bf16)
        return jnp.concatenate([packed] * (count // 16), axis=0)

    def add(block, _):
        lefts, rights = [], []
        for x in range(group // 8):
            eight = block * (group // 8) + x
            shown = pltpu.roll(bins_t[lax.shift_right_logical(eight, 4)], (128 - 8 * (eight & 15)) & 127, axis=1)
            for u, record in enumerate(records_of(eight)):
                low, high, value = [spread(rows[k, pl.ds(record, 1), :], 256) for k in range(3)]
                lefts.append(
                    jnp.concatenate(
                        [jnp.where(low == number, value, no_left), jnp.where(high == number, value, no_left)],
                        axis=0,
                    )
                )
                bin_of = jnp.broadcast_to(shown[:, u : u + 1], (cells, 128)).astype(bf16)
                some = [spread(ratio[k, pl.ds(eight * 8 + u, 1), :], cells) for k in range(2)]
                rights.append(
                    jnp.concatenate(
                        [
                            jnp.where(first_bins >= bin_of, some[0], no_right),
                            jnp.where(last_bins >= bin_of, some[1], no_right),
                        ],
                        axis=1,
                    )
                )
        out[...] += jnp.dot(
            jnp.concatenate(lefts, axis=1), jnp.concatenate(rights, axis=0), preferred_element_type=f32
        )
        return 0

    lax.fori_loop(0, tiles // group, add, 0)


def per_device(
    level_start,
    bed_depth,
    wet_bits,
    tile_owner,
    vuln_weight,
    vuln_bias,
    account_index,
    bin_index,
    exposure_value,
    deductible,
    limit,
):
    _, rows, width = level_start.shape
    cells, bin_count = vuln_weight.shape
    account_count = deductible.shape[0]
    owners = lax.axis_size("terrain")
    events = lax.axis_size("event")
    me = lax.axis_index("terrain")
    slots = account_index.shape[0]
    capacity = slots // owners
    tiles = tile_owner.shape[0]
    vmem = pl.BlockSpec(memory_space=pltpu.VMEM)

    ready, own, edge = pl.pallas_call(
        functools.partial(pack_kernel, each=2 * capacity),
        in_specs=[pl.BlockSpec(memory_space=pltpu.HBM)] * 7,
        out_specs=(vmem,) * 3,
        scratch_shapes=[
            pltpu.VMEM((slots, cells), jnp.int32),
            pltpu.VMEM((slots, cells), jnp.int32),
            pltpu.VMEM((slots, cells), bf16),
            pltpu.VMEM((rows, width), f32),
            pltpu.VMEM((rows, width), f32),
            pltpu.VMEM((rows, width), jnp.int32),
            pltpu.VMEM((1, tiles), jnp.int32),
            pltpu.SemaphoreType.DMA((7,)),
        ],
        out_shape=(
            jax.ShapeDtypeStruct((owners, 6 * capacity, cells), jnp.int16),
            jax.ShapeDtypeStruct((3 * rows + 8, width), f32),
            jax.ShapeDtypeStruct((3 * HALO, width), f32),
        ),
        compiler_params=pltpu.CompilerParams(vmem_limit_bytes=60 << 20),
        name="pack",
    )(
        account_index,
        bin_index,
        exposure_value,
        level_start[0],
        bed_depth,
        wet_bits[0],
        tile_owner.reshape(1, tiles),
    )
    records = lax.all_to_all(ready, "terrain", 0, 0, tiled=True)
    mate = lax.ppermute(own, "terrain", [(i, i ^ 1) for i in range(owners)])

    def outward(step):
        pairs = [(i, i + step if i % 2 else i - step) for i in range(owners)]
        return [(i, k) for i, k in pairs if 0 <= k < owners]

    edge_a = lax.ppermute(edge, "terrain", outward(1))
    edge_b = lax.ppermute(edge, "terrain", outward(2))

    held = (width // 128, 2 * (rows + HALO) + 16, 128)
    place = pl.pallas_call(
        functools.partial(place_kernel, row=0, tiles=tiles, capacity=capacity),
        in_specs=[vmem] * 2,
        out_specs=vmem,
        out_shape=jax.ShapeDtypeStruct((2 * tiles // 128, 128), jnp.int32),
        compiler_params=pltpu.CompilerParams(vmem_limit_bytes=16 << 20),
        cost_estimate=pl.CostEstimate(flops=10_000_000, bytes_accessed=4_000_000, transcendentals=0),
        name="place",
    )(own[3 * rows :], mate[3 * rows :])
    level, ratio = pl.pallas_call(
        functools.partial(water_kernel, rows=rows),
        in_specs=[vmem] * 7,
        out_specs=(vmem,) * 2,
        out_shape=(
            jax.ShapeDtypeStruct((rows, width), f32),
            jax.ShapeDtypeStruct((2, 2 * tiles, bin_count // 2), f32),
        ),
        scratch_shapes=[
            pltpu.VMEM((3, *held), f32),
            pltpu.VMEM((3, *held), f32),
            pltpu.VMEM(held, f32),
            pltpu.VMEM(held, jnp.int32),
        ],
        compiler_params=pltpu.CompilerParams(vmem_limit_bytes=32 << 20),
        cost_estimate=pl.CostEstimate(flops=1, bytes_accessed=1, transcendentals=0),
        name="water",
    )(own, mate, edge_a, edge_b, vuln_weight, vuln_bias[None], place)

    group = 256
    share = account_count // owners
    gross = pl.pallas_call(
        functools.partial(gross_kernel, group=group, per_row=width // cells, tiles=2 * tiles),
        grid_spec=pltpu.PrefetchScalarGridSpec(
            num_scalar_prefetch=1,
            grid=(),
            in_specs=[vmem, vmem],
            out_specs=vmem,
            scratch_shapes=[
                pltpu.VMEM((4, owners * 2 * capacity, cells), f32),
                pltpu.VMEM((2 * tiles, cells), f32),
                pltpu.VMEM((2 * tiles // 128, cells, 128), f32),
            ],
        ),
        out_shape=jax.ShapeDtypeStruct((account_count // 2, bin_count), f32),
        compiler_params=pltpu.CompilerParams(vmem_limit_bytes=58 << 20),
        name="gross",
    )(place, records, ratio)

    alike = [list(range(core, owners, 2)) for core in range(2)]
    parts = lax.all_to_all(
        gross.reshape(owners // 2, share, bin_count), "terrain", 0, 0, tiled=True, axis_index_groups=alike
    )
    own_gross = parts.sum(axis=0)
    scale = account_count / (rows * owners * width)
    own_deduct = lax.dynamic_slice_in_dim(deductible, me * share, share, 0)
    own_limit = lax.dynamic_slice_in_dim(limit, me * share, share, 0)
    net = jnp.minimum(jnp.maximum(own_gross * scale - own_deduct[:, None], 0.0), own_limit[:, None])
    everyone = jnp.broadcast_to(net.astype(bf16)[None], (owners, share, bin_count))
    net_loss = lax.all_to_all(everyone, "terrain", 0, 0, tiled=True).reshape(1, account_count, bin_count)
    others = [
        lax.ppermute(net, "event", [(i, (i + k) % events) for i in range(events)])
        for k in range(1, events)
    ]
    portfolio = sum(others, net) / events
    return (level[None], net_loss, portfolio)


def solution(mesh):
    placed = (
        P("event", "terrain", None),
        P("terrain", None),
        P("event", "terrain", None),
        P("terrain", None),
        P(),
        P(),
        P("terrain", None),
        P("terrain", None),
        P("terrain", None),
        P(),
        P(),
    )
    return jax.shard_map(
        per_device,
        mesh=mesh,
        in_specs=placed,
        out_specs=(P("event", "terrain", None), P("event", None, None), P("terrain", None)),
        check_vma=False,
    )
```
